32 devices in a mesh: groups: 2 (over x), out: 16 (over z, y, core).
Axes of the slice: x: 2, y: 2, z: 4, core: 2. Of those that a mesh axis runs over, the one named last changes fastest.
Arguments:
- tokens: bfloat16 [256, 8192], P('groups', 'out'), parts along dimension 0, may hold values from -60 to 60, as said below
- grad_hidden: bfloat16 [256, 16384], P('groups', 'out'), parts along dimension 0, may hold values from -6 to 6
- w_gate: bfloat16 [8192, 16384], P(None, 'out'), may hold values from -0.0625 to 0.0625
- w_up: bfloat16 [8192, 16384], P(None, 'out'), may hold values from -0.0625 to 0.0625
- a_factors: bfloat16 [8192, 128], replicated, may hold values from -0.0625 to 0.0625
- b_factors: bfloat16 [2, 64, 16384], P(None, None, 'out'), may hold values from -0.75 to 0.75
- magnitudes: float32 [2, 16384], P(None, 'out'), may hold values from 1 to 2
Outputs:
- hidden: bfloat16 [256, 16384], P('groups', 'out'), parts along dimension 0
- grad_tokens: bfloat16 [256, 8192], P('groups', 'out'), parts along dimension 0
- step_a: float32 [16384, 128], P(('groups', 'out')), parts along dimension 0
- step_b: float32 [4, 64, 16384], P('groups', None, 'out'), parts along dimension 0
- step_m: float32 [4, 16384], P('groups', 'out'), parts along dimension 0
The draws below stay inside these ranges and needn't reach their ends.
There are 2 independent parts, one for each index of `groups`. The reference program is written for one: setup_inputs(seed, part) draws one part's arguments, and reference() takes and returns one part's arrays. A program takes and returns all parts, laid end to end along the dimension named above; an argument that names none is the same for every part. Nothing has to cross between parts.
Inputs may be any that keep to these rules, and one draw needn't show every extreme that they name: `tokens`: activations with feature scales that differ between features.
All inputs are finite; a program needn't handle non-finite values.
Results may differ from the reference program's by a relative error of at most 0.0073.
Values may be sent and summed in bfloat16 or wider, within the bound.
A program may use at most 128 MiB of HBM per device.

```python
import jax
import jax.numpy as jnp
from jax import lax

D = 8192
FW = 16384
R = 64
TOKENS = 128


def draw_tokens(key, part):
    first_key = jax.random.fold_in(jax.random.fold_in(key, 11), 0)
    channel = 3.0 ** (jnp.arange(D, dtype=jnp.float32) / max(D - 1, 1))
    values = jnp.clip(jax.random.normal(first_key, (TOKENS, D), jnp.float32), -5.0, 5.0)
    return (values * channel[None, :]).astype(jnp.bfloat16)


def shard_levels(key, shape, cuts, smallest, high):
    def one(axis_at, blocks):
        steps = jax.random.uniform(jax.random.fold_in(jax.random.fold_in(key, 6), axis_at), (blocks,), jnp.float32, smallest / len(cuts), high / len(cuts))
        return jnp.repeat(jnp.exp(steps), shape[axis_at] // blocks).reshape((-1,) + (1,) * (len(shape) - axis_at - 1))

    factor_of = one(*cuts[0])
    for cut in cuts[1:]:
        factor_of = factor_of * one(*cut)
    return factor_of


def bell_draw(stream_key, dims, deviation, reach, pieces=(), kind=jnp.bfloat16):
    gain = shard_levels(stream_key, dims, pieces, -0.22, 0.18) if pieces else 1.0
    array = jax.random.normal(stream_key, dims, jnp.float32) * deviation * gain
    return jnp.minimum(jnp.maximum(array, -reach), reach).astype(kind)


def setup_inputs(seed: int = 0, part: int = 0) -> dict:
    splits = jax.random.split(jax.random.key(seed), 8)
    own_keys = jax.random.split(jax.random.fold_in(splits[7], part), 8)
    return {
        "tokens": draw_tokens(jax.random.fold_in(jax.random.fold_in(splits[7], part), 71), part),
        "grad_hidden": bell_draw(own_keys[1], (TOKENS, FW), 1.0, 6.0, ((1, 16),)),
        "w_gate": bell_draw(splits[2], (D, FW), D ** -0.5, 0.0625, ((1, 16),)),
        "w_up": bell_draw(splits[3], (D, FW), D ** -0.5, 0.0625, ((1, 16),)),
        "a_factors": bell_draw(splits[4], (D, 2 * R), D ** -0.5, 0.0625),
        "b_factors": bell_draw(splits[5], (2, R, FW), R ** -0.5, 0.75, ((2, 16),)),
        "magnitudes": jnp.clip(1.0 + 1.0 * jax.random.uniform(splits[6], (2, FW), jnp.float32) ** shard_levels(splits[6], (2, FW), ((1, 16),), -0.2, 0.2), 1.0, 2.0),
    }


def reference(tokens, grad_hidden, w_gate, w_up, a_factors, b_factors, magnitudes):
    weights = (w_gate, w_up)
    low = jnp.dot(tokens, a_factors, preferred_element_type=jnp.float32).astype(jnp.bfloat16)
    norms = []
    scales = []
    bases = []
    pres = []
    for which in range(2):
        left = a_factors[:, which * R:(which + 1) * R]
        right = b_factors[which]
        merged = weights[which].astype(jnp.float32) + jnp.dot(left, right, preferred_element_type=jnp.float32)
        norm_col = jnp.sqrt(lax.optimization_barrier(jnp.sum(merged * merged, axis=0)) + 1e-06)
        scale = magnitudes[which] / norm_col
        base = jnp.dot(tokens, weights[which], preferred_element_type=jnp.float32)
        base = base + jnp.dot(low[:, which * R:(which + 1) * R], right, preferred_element_type=jnp.float32)
        norms.append(norm_col)
        scales.append(scale)
        bases.append(base)
        pres.append(base * scale[None, :])
    sigma = jax.nn.sigmoid(pres[0])
    hidden = (pres[0] * sigma * pres[1]).astype(jnp.bfloat16)
    cotangent = grad_hidden.astype(jnp.float32)
    dpres = (cotangent * pres[1] * sigma * (1.0 + pres[0] * (1.0 - sigma)), cotangent * pres[0] * sigma)
    partial_sum = jnp.zeros((tokens.shape[0], tokens.shape[1]), jnp.float32)
    z_blocks = []
    grad_bs = []
    grad_ms = []
    for which in range(2):
        dscaled = (dpres[which] * scales[which][None, :]).astype(jnp.bfloat16)
        grad_ms.append(lax.optimization_barrier(jnp.sum(dpres[which] * bases[which], axis=0)) / norms[which])
        grad_bs.append(jnp.dot(low[:, which * R:(which + 1) * R].T, dscaled, preferred_element_type=jnp.float32))
        z_blocks.append(jnp.dot(dscaled, b_factors[which].T, preferred_element_type=jnp.float32))
        partial_sum = partial_sum + jnp.dot(dscaled, weights[which].T, preferred_element_type=jnp.float32)
    z_all = jnp.concatenate(z_blocks, axis=1)
    a_wide = a_factors.astype(jnp.float32)
    grad_tokens = (partial_sum + jnp.dot(z_all, a_wide.T, precision=lax.Precision.HIGHEST)).astype(jnp.bfloat16)
    grad_a = jnp.dot(tokens.astype(jnp.float32).T, z_all, precision=lax.Precision.HIGHEST)
    grad_b = jnp.stack(grad_bs)
    grad_m = jnp.stack(grad_ms)
    energy = jnp.sum(grad_a * grad_a) + jnp.sum(grad_b * grad_b) + jnp.sum(grad_m * grad_m)
    count_all = 2 * D * R + 2 * R * FW + 2 * FW
    rms_value = jnp.sqrt(energy / count_all + 1e-06)
    return (hidden, grad_tokens, grad_a / rms_value, grad_b / rms_value, grad_m / rms_value)
```

```python
import jax
import jax.numpy as jnp
from jax import lax
from jax.sharding import PartitionSpec as P

D = 8192
FW = 16384
R = 64


def inner_product(left_side, right_side, precision=None):
    return lax.dot_general(
        left_side,
        right_side,
        (((0,), (0,)), ((), ())),
        precision=precision,
        preferred_element_type=jnp.float32,
    )


def outer_contract(left_side, right_side, precision=None):
    return lax.dot_general(
        left_side,
        right_side,
        (((1,), (1,)), ((), ())),
        precision=precision,
        preferred_element_type=jnp.float32,
    )


def split_parts(values):
    upper = values.astype(jnp.bfloat16)
    lower = (values - upper.astype(jnp.float32)).astype(jnp.bfloat16)
    return (upper, lower)


def per_device(tokens, grad_hidden, w_gate, w_up, a_factors, b_factors, magnitudes):
    weights = (w_gate, w_up)
    rank = a_factors.shape[1] // 2
    count_tokens = tokens.shape[0]
    norms = []
    scales = []
    for which in range(2):
        weight = weights[which]
        left = a_factors[:, which * rank : (which + 1) * rank]
        right = b_factors[which]
        merged = weight.astype(jnp.float32) + jnp.dot(
            left, right, preferred_element_type=jnp.float32
        )
        squares = jnp.sum(merged * merged, axis=0)
        norm_col = jnp.sqrt(squares + 1e-06)
        norms.append(norm_col)
        scales.append(magnitudes[which] / norm_col)
    whole = lax.all_gather(tokens, "out", axis=1, tiled=True)
    base_gate = jnp.dot(whole, w_gate, preferred_element_type=jnp.float32)
    base_up = jnp.dot(whole, w_up, preferred_element_type=jnp.float32)
    low_wide = jnp.dot(whole, a_factors, preferred_element_type=jnp.float32)
    low = low_wide.astype(jnp.bfloat16)
    bases = []
    pres = []
    for which, raw in enumerate((base_gate, base_up)):
        base = raw + jnp.dot(
            low[:, which * rank : (which + 1) * rank],
            b_factors[which],
            preferred_element_type=jnp.float32,
        )
        bases.append(base)
        pres.append(base * scales[which][None, :])
    sigma = jax.nn.sigmoid(pres[0])
    hidden = (pres[0] * sigma * pres[1]).astype(jnp.bfloat16)
    cotangent = grad_hidden.astype(jnp.float32)
    dpres = (
        cotangent * pres[1] * sigma * (1.0 + pres[0] * (1.0 - sigma)),
        cotangent * pres[0] * sigma,
    )
    partial_sum = jnp.zeros((count_tokens, w_gate.shape[0]), jnp.float32)
    z_blocks = []
    grad_bs = []
    grad_ms = []
    for which in range(2):
        dscaled = (dpres[which] * scales[which][None, :]).astype(jnp.bfloat16)
        grad_ms.append(jnp.sum(dpres[which] * bases[which], axis=0) / norms[which])
        grad_bs.append(inner_product(low[:, which * rank : (which + 1) * rank], dscaled))
        z_blocks.append(outer_contract(dscaled, b_factors[which]))
        partial_sum = partial_sum + outer_contract(dscaled, weights[which])
    z_local = jnp.concatenate(z_blocks, axis=1)
    grad_b = jnp.stack(grad_bs)
    grad_m = jnp.stack(grad_ms)
    summed_inputs = lax.psum_scatter(partial_sum, "out", scatter_dimension=1, tiled=True)
    local_energy = jnp.sum(grad_b * grad_b) + jnp.sum(grad_m * grad_m)
    z_all, small_energy = lax.psum((z_local, local_energy), "out")
    z_upper, z_lower = split_parts(z_all)
    full_a = inner_product(whole, z_upper) + inner_product(whole, z_lower)
    grad_a = inner_product(tokens, z_upper) + inner_product(tokens, z_lower)
    mine = tokens.shape[1]
    a_mine = lax.dynamic_slice_in_dim(a_factors, lax.axis_index("out") * mine, mine, 0)
    adapter = outer_contract(z_upper, a_mine) + outer_contract(z_lower, a_mine)
    grad_tokens = (summed_inputs + adapter).astype(jnp.bfloat16)
    energy = small_energy + jnp.sum(full_a * full_a)
    count_all = 2 * D * R + 2 * R * FW + 2 * FW
    rms_value = jnp.sqrt(energy / count_all + 1e-06)
    return (hidden, grad_tokens, grad_a / rms_value, grad_b / rms_value, grad_m / rms_value)


def solution(mesh):
    in_specs = (
        P("groups", "out"),
        P("groups", "out"),
        P(None, "out"),
        P(None, "out"),
        P(),
        P(None, None, "out"),
        P(None, "out"),
    )
    out_specs = (
        P("groups", "out"),
        P("groups", "out"),
        P(("groups", "out"), None),
        P("groups", None, "out"),
        P("groups", "out"),
    )
    return jax.shard_map(
        per_device, mesh=mesh, in_specs=in_specs, out_specs=out_specs, check_vma=False
    )
```

```python
import functools

import jax
import jax.numpy as jnp
from jax import lax
from jax.experimental import pallas as pl
from jax.experimental.pallas import tpu as pltpu
from jax.sharding import PartitionSpec as P

F32 = jnp.float32
BF16 = jnp.bfloat16


def mm(left, right):
    return lax.dot_general(left, right, (((1,), (0,)), ((), ())), preferred_element_type=F32)


def mm_t(left, right):
    return lax.dot_general(left, right, (((1,), (1,)), ((), ())), preferred_element_type=F32)


def split_parts(values):
    upper = values.astype(BF16)
    lower = (values - upper.astype(F32)).astype(BF16)
    return upper, lower


def fold_rows(values):
    rows, cols = values.shape
    return jnp.sum(values.reshape(rows // 8, 8, cols), axis=0)


def kernel(
    n, tok, gh, wg, wu, a, b, mag,
    hidden, gtok, step_a, step_b, step_m,
    wbuf, gat, bpad, sq, base, low, ds, own, sc, rc, sm, rm, sh, rh, z0, zc, z1, zm, zh,
    w_sem, ga_send, ga_recv, c_send, c_recv, m_send, m_recv, h_send, h_recv, z_send, z_recv,
):
    nh = n // 4
    width = a.shape[1]
    rank = width // 2
    depth = a.shape[0]
    block = depth // n
    cols = gh.shape[1]
    tokens = tok.shape[0]
    me = lax.axis_index("out")
    core = lax.rem(me, 2)
    mid = lax.rem(me // 2, 2)
    hi = me // 4

    def place(h, m, c):
        return (h * 2 + m) * 2 + c

    core_peer = place(hi, mid, 1 - core)
    mid_peer = place(hi, 1 - mid, core)

    def hi_after(k):
        return lax.rem(hi + 1 + k, nh)

    def hi_before(k):
        return lax.rem(hi + 2 * nh - 1 - k, nh)

    def remote(src, dst, send, recv, target):
        return pltpu.make_async_remote_copy(
            src_ref=src, dst_ref=dst, send_sem=send, recv_sem=recv,
            device_id={"out": target}, device_id_type=pl.DeviceIdType.MESH,
        )

    def rows_of(j):
        return pl.ds(pl.multiple_of(j * block, block), block)

    def weight_copy(which, j):
        source = wg if which == 0 else wu
        return pltpu.make_async_copy(
            source.at[rows_of(j), :], wbuf.at[which, rows_of(j), :], w_sem.at[which, j]
        )

    @pl.loop(0, n)
    def _(j):
        weight_copy(0, j).start()
        weight_copy(1, j).start()

    barrier = pltpu.get_barrier_semaphore()
    peers = [core_peer, mid_peer] + [place(hi_after(k), mid, core) for k in range(nh - 1)]
    for peer in peers:
        pl.semaphore_signal(
            barrier, inc=1, device_id={"out": peer}, device_id_type=pl.DeviceIdType.MESH
        )
    pl.semaphore_wait(barrier, len(peers))

    pending = []
    count = [0]

    def gather_send(src, origin, target):
        copy = remote(src, gat.at[origin], ga_send.at[count[0]], ga_recv.at[origin], target)
        count[0] += 1
        copy.start()
        pending.append(copy)

    def gather_wait(origin):
        remote(gat.at[origin], gat.at[origin], ga_send.at[0], ga_recv.at[origin], core_peer).wait_recv()

    gather_send(tok, me, mid_peer)
    for k in range(nh - 1):
        gather_send(tok, me, place(hi_after(k), mid, core))
    gather_send(tok, me, core_peer)
    gat[me] = tok[...]

    bpad[...] = jnp.zeros_like(bpad)
    bpad[0, :rank, :] = b[0]
    bpad[1, rank:, :] = b[1]
    sq[...] = jnp.zeros_like(sq)

    events = {}

    def from_hi(k):
        origin = place(hi_before(k), mid, core)
        gather_wait(origin)
        gather_send(gat.at[origin], origin, mid_peer)
        gather_send(gat.at[origin], origin, core_peer)

    def from_mid(k):
        origin = place(hi if k == 0 else hi_before(k - 1), 1 - mid, core)
        gather_wait(origin)
        gather_send(gat.at[origin], origin, core_peer)

    for k in range(nh - 1):
        events.setdefault(n // 4 + (k * n) // (2 * nh), []).append(functools.partial(from_hi, k))
    for k in range(nh):
        events.setdefault(min(n, n * 5 // 16 + (k * n * 3) // (4 * nh)), []).append(
            functools.partial(from_mid, k)
        )

    part = min(128, block)

    def norm_step(j):
        for which in range(2):
            weight_copy(which, j).wait()

        @pl.loop(0, block // part)
        def _(i):
            rows = pl.ds(pl.multiple_of(j * block + i * part, part), part)
            left = a[rows, :]
            for which in range(2):
                merged = wbuf[which, rows, :].astype(F32) + mm(left, bpad[which])
                sq[which] += fold_rows(merged * merged)

    marks = sorted(set([0, n] + list(events)))
    for start, end in zip(marks, marks[1:] + [None]):
        for event in events.get(start, []):
            event()
        if end is not None:
            pl.loop(start, end)(norm_step)

    base[...] = jnp.zeros_like(base)
    low[...] = jnp.zeros_like(low)

    def forward(j):
        x = gat[j]
        for which in range(2):
            base[which] += mm(x, wbuf[which, rows_of(j), :])
        low[...] += mm(x, a[rows_of(j), :])

    @pl.loop(0, n // 2)
    def _(q):
        forward(2 * q + core)

    @pl.loop(0, n // 2)
    def _(q):
        origin = 2 * q + 1 - core
        gather_wait(origin)
        forward(origin)

    low_bf = low[...].astype(BF16)
    low_t = jnp.transpose(low[...]).astype(BF16)
    piece = min(256, cols)
    for c0 in range(0, cols, piece):
        cut = slice(c0, c0 + piece)
        norms, scales, bases, pres = [], [], [], []
        for which in range(2):
            norm = jnp.sqrt(jnp.sum(sq[which, :, cut], axis=0, keepdims=True) + 1e-06)
            norms.append(norm)
            scales.append(mag[which : which + 1, cut] / norm)
            bases.append(base[which, :, cut] + mm(low_bf, bpad[which, :, cut]))
            pres.append(bases[which] * scales[which])
        sigma = 1.0 / (1.0 + jnp.exp(-pres[0]))
        hidden[:, cut] = (pres[0] * sigma * pres[1]).astype(BF16)
        cot = gh[:, cut].astype(F32)
        dpres = (
            cot * pres[1] * sigma * (1.0 + pres[0] * (1.0 - sigma)),
            cot * pres[0] * sigma,
        )
        for which in range(2):
            dscaled = (dpres[which] * scales[which]).astype(BF16)
            ds[which, :, cut] = dscaled
            step_m[which : which + 1, cut] = (
                jnp.sum(dpres[which] * bases[which], axis=0, keepdims=True) / norms[which]
            )
            step_b[which, :, cut] = mm(low_t[which * rank : (which + 1) * rank, :], dscaled)

    z0[:tokens, :] = mm_t(ds[0], bpad[0]) + mm_t(ds[1], bpad[1])
    lanes = jnp.zeros((8, width), F32)
    for c0 in range(0, cols, width):
        for which in range(2):
            value = step_b[which, :, c0 : c0 + width]
            lanes += fold_rows(value * value)
            line = step_m[which : which + 1, c0 : c0 + width]
            lanes += jnp.where(
                lax.broadcasted_iota(jnp.int32, (8, width), 0) == 0, line * line, 0.0
            )
    z0[tokens:, :] = lanes

    def start(copy):
        copy.start()
        pending.append(copy)
        return copy

    z_core = start(remote(z0, zc, z_send.at[0], z_recv.at[0], core_peer))

    def partial(j):
        return mm_t(ds[0], wbuf[0, rows_of(j), :]) + mm_t(ds[1], wbuf[1, rows_of(j), :])

    core_copies, mid_copies, hi_copies, z_hi = [], [], [], []
    z_mid = []

    def core_stage(i):
        core_copies[i].wait_recv()
        total = own[i] + rc[i].astype(F32)
        if i < nh:
            sm[i] = total.astype(BF16)
            mid_copies.append(start(remote(sm.at[i], rm.at[i], m_send.at[i], m_recv.at[i], mid_peer)))
        else:
            own[i] = total

    def mid_stage(k):
        mid_copies[k].wait_recv()
        total = own[nh + k] + rm[k].astype(F32)
        if k < nh - 1:
            sh[k] = total.astype(BF16)
            hi_copies.append(
                start(
                    remote(
                        sh.at[k], rh.at[k], h_send.at[k], h_recv.at[k],
                        place(hi_after(k), mid, core),
                    )
                )
            )
        else:
            own[nh + k] = total

    for i in range(2 * nh):
        m = 1 - mid if i < nh else mid
        h = hi_after(i % nh)
        sc[i] = partial(place(h, m, 1 - core)).astype(BF16)
        core_copies.append(start(remote(sc.at[i], rc.at[i], c_send.at[i], c_recv.at[i], core_peer)))
        own[i] = partial(place(h, m, core))
        if i >= 1:
            core_stage(i - 1)
        if i == 1:
            z_core.wait_recv()
            z1[...] = z0[...] + zc[...]
            z_mid.append(start(remote(z1, zm, z_send.at[1], z_recv.at[1], mid_peer)))
        if i == 3:
            z_mid[0].wait_recv()
            zh[hi] = z1[...] + zm[...]
            for k in range(nh - 1):
                z_hi.append(
                    start(
                        remote(
                            zh.at[hi], zh.at[hi], z_send.at[2 + k], z_recv.at[2 + k],
                            place(hi_after(k), mid, core),
                        )
                    )
                )
        if i == nh + 2:
            mid_stage(0)
    core_stage(2 * nh - 1)
    for k in range(1, nh):
        mid_stage(k)

    for k in range(nh - 1):
        slot = hi_before(k)
        remote(zh.at[slot], zh.at[slot], z_send.at[2 + k], z_recv.at[2 + k], core_peer).wait_recv()
    z_sum = zh[0]
    for k in range(1, nh):
        z_sum = z_sum + zh[k]
    z_upper, z_lower = split_parts(z_sum[:tokens, :])
    z_t = jnp.transpose(z_sum[:tokens, :])
    t_upper, t_lower = split_parts(z_t)
    sq[0, :, :width] = z_sum[tokens:, :]

    @pl.loop(0, n)
    def _(j):
        x = gat[j]
        grad = mm(t_upper, x) + mm(t_lower, x)
        folded = fold_rows(grad * grad)
        total = folded[:, :width]
        for c0 in range(width, block, width):
            total += folded[:, c0 : c0 + width]
        sq[0, :, :width] += total

    energy = jnp.sum(jnp.sum(sq[0, :, :width], axis=0, keepdims=True), axis=1, keepdims=True)
    entries = depth * width + 2 * rank * cols * n + 2 * cols * n
    inverse = 1.0 / jnp.sqrt(energy / entries + 1e-06)
    mine = tok[...]
    step_a[...] = jnp.transpose((mm(t_upper, mine) + mm(t_lower, mine)) * inverse)
    step_b[...] = step_b[...] * inverse.reshape(1, 1, 1)
    step_m[...] = step_m[...] * inverse
    a_mine = a[rows_of(me), :]
    total = own[2 * nh - 1] + mm_t(z_upper, a_mine) + mm_t(z_lower, a_mine)
    for k in range(nh - 1):
        hi_copies[k].wait_recv()
        total += rh[k].astype(F32)
    gtok[...] = total.astype(BF16)
    for copy in pending:
        copy.wait_send()


def per_device(n, tokens, grad_hidden, w_gate, w_up, a_factors, b_factors, magnitudes):
    count, block = tokens.shape
    depth, cols = w_gate.shape
    width = a_factors.shape[1]
    nh = n // 4
    vmem = pl.BlockSpec(memory_space=pltpu.VMEM)
    hbm = pl.BlockSpec(memory_space=pl.ANY)
    dma = pltpu.SemaphoreType.DMA
    z_shape = (count + 8, width)
    return pl.pallas_call(
        functools.partial(kernel, n),
        out_shape=(
            jax.ShapeDtypeStruct((count, cols), BF16),
            jax.ShapeDtypeStruct((count, block), BF16),
            jax.ShapeDtypeStruct((block, width), F32),
            jax.ShapeDtypeStruct((2, width // 2, cols), F32),
            jax.ShapeDtypeStruct((2, cols), F32),
        ),
        in_specs=[vmem, vmem, hbm, hbm, vmem, vmem, vmem],
        out_specs=(vmem,) * 5,
        scratch_shapes=[
            pltpu.VMEM((2, depth, cols), BF16),
            pltpu.VMEM((n, count, block), BF16),
            pltpu.VMEM((2, width, cols), BF16),
            pltpu.VMEM((2, 8, cols), F32),
            pltpu.VMEM((2, count, cols), F32),
            pltpu.VMEM((count, width), F32),
            pltpu.VMEM((2, count, cols), BF16),
            pltpu.VMEM((2 * nh, count, block), F32),
            pltpu.VMEM((2 * nh, count, block), BF16),
            pltpu.VMEM((2 * nh, count, block), BF16),
            pltpu.VMEM((nh, count, block), BF16),
            pltpu.VMEM((nh, count, block), BF16),
            pltpu.VMEM((nh - 1, count, block), BF16),
            pltpu.VMEM((nh - 1, count, block), BF16),
            pltpu.VMEM(z_shape, F32),
            pltpu.VMEM(z_shape, F32),
            pltpu.VMEM(z_shape, F32),
            pltpu.VMEM(z_shape, F32),
            pltpu.VMEM((nh,) + z_shape, F32),
            dma((2, n)),
            dma((n,)),
            dma((n,)),
            dma((2 * nh,)),
            dma((2 * nh,)),
            dma((nh,)),
            dma((nh,)),
            dma((nh - 1,)),
            dma((nh - 1,)),
            dma((nh + 1,)),
            dma((nh + 1,)),
        ],
        compiler_params=pltpu.CompilerParams(
            collective_id=0, has_side_effects=True, vmem_limit_bytes=60 * 1024 * 1024
        ),
    )(tokens, grad_hidden, w_gate, w_up, a_factors, b_factors, magnitudes)


def solution(mesh):
    in_specs = (
        P("groups", "out"),
        P("groups", "out"),
        P(None, "out"),
        P(None, "out"),
        P(),
        P(None, None, "out"),
        P(None, "out"),
    )
    out_specs = (
        P("groups", "out"),
        P("groups", "out"),
        P(("groups", "out"), None),
        P("groups", None, "out"),
        P("groups", "out"),
    )
    return jax.shard_map(
        functools.partial(per_device, mesh.shape["out"]),
        mesh=mesh, in_specs=in_specs, out_specs=out_specs, check_vma=False,
    )
```

```python
import functools

import jax
import jax.numpy as jnp
from jax import lax
from jax.experimental import pallas as pl
from jax.experimental.pallas import tpu as pltpu
from jax.sharding import PartitionSpec as P

F32 = jnp.float32
BF16 = jnp.bfloat16


def mm(left, right):
    return lax.dot_general(left, right, (((1,), (0,)), ((), ())), preferred_element_type=F32)


def mm_t(left, right):
    return lax.dot_general(left, right, (((1,), (1,)), ((), ())), preferred_element_type=F32)


def split_parts(values):
    upper = values.astype(BF16)
    lower = (values - upper.astype(F32)).astype(BF16)
    return upper, lower


def fold_rows(values):
    rows, cols = values.shape
    return jnp.sum(values.reshape(rows // 8, 8, cols), axis=0)


def kernel(
    n, tok, gh, wg, wu, a, b, mag,
    hidden, gtok, step_a, step_b, step_m,
    wbuf, gat, bpad, sq, base, low, ds, own, sc, rc, sm, rm, sh, rh, z0, zc, z1, zm, zh,
    w_sem, ga_send, ga_recv, c_send, c_recv, m_send, m_recv, h_send, h_recv, z_send, z_recv,
):
    nh = n // 4
    width = a.shape[1]
    rank = width // 2
    depth = a.shape[0]
    block = depth // n
    cols = gh.shape[1]
    tokens = tok.shape[0]
    me = lax.axis_index("out")
    core = lax.rem(me, 2)
    mid = lax.rem(me // 2, 2)
    hi = me // 4

    def place(h, m, c):
        return (h * 2 + m) * 2 + c

    core_peer = place(hi, mid, 1 - core)
    mid_peer = place(hi, 1 - mid, core)

    def hi_after(k):
        return lax.rem(hi + 1 + k, nh)

    def hi_before(k):
        return lax.rem(hi + 2 * nh - 1 - k, nh)

    def remote(src, dst, send, recv, target):
        return pltpu.make_async_remote_copy(
            src_ref=src, dst_ref=dst, send_sem=send, recv_sem=recv,
            device_id={"out": target}, device_id_type=pl.DeviceIdType.MESH,
        )

    def rows_of(j):
        return pl.ds(pl.multiple_of(j * block, block), block)

    def weight_copy(which, j):
        source = wg if which == 0 else wu
        return pltpu.make_async_copy(
            source.at[rows_of(j), :], wbuf.at[which, rows_of(j), :], w_sem.at[which, j]
        )

    @pl.loop(0, n)
    def _(j):
        weight_copy(0, j).start()
        weight_copy(1, j).start()

    barrier = pltpu.get_barrier_semaphore()
    peers = [core_peer, mid_peer] + [place(hi_after(k), mid, core) for k in range(nh - 1)]
    for peer in peers:
        pl.semaphore_signal(
            barrier, inc=1, device_id={"out": peer}, device_id_type=pl.DeviceIdType.MESH
        )
    pl.semaphore_wait(barrier, len(peers))

    pending = []
    count = [0]

    def gather_send(src, origin, target):
        copy = remote(src, gat.at[origin], ga_send.at[count[0]], ga_recv.at[origin], target)
        count[0] += 1
        copy.start()
        pending.append(copy)

    def gather_wait(origin):
        remote(gat.at[origin], gat.at[origin], ga_send.at[0], ga_recv.at[origin], core_peer).wait_recv()

    gather_send(tok, me, mid_peer)
    for k in range(nh - 1):
        gather_send(tok, me, place(hi_after(k), mid, core))
    gather_send(tok, me, core_peer)
    gat[me] = tok[...]

    bpad[...] = jnp.zeros_like(bpad)
    bpad[0, :rank, :] = b[0]
    bpad[1, rank:, :] = b[1]
    sq[...] = jnp.zeros_like(sq)

    events = {}

    def from_hi(k):
        origin = place(hi_before(k), mid, core)
        gather_wait(origin)
        gather_send(gat.at[origin], origin, mid_peer)
        gather_send(gat.at[origin], origin, core_peer)

    def from_mid(k):
        origin = place(hi if k == 0 else hi_before(k - 1), 1 - mid, core)
        gather_wait(origin)
        gather_send(gat.at[origin], origin, core_peer)

    for k in range(nh - 1):
        events.setdefault(n // 4 + (k * n) // (2 * nh), []).append(functools.partial(from_hi, k))
    for k in range(nh):
        events.setdefault(min(n, n * 5 // 16 + (k * n * 3) // (4 * nh)), []).append(
            functools.partial(from_mid, k)
        )

    part = min(128, block)

    def norm_step(j):
        for which in range(2):
            weight_copy(which, j).wait()

        @pl.loop(0, block // part)
        def _(i):
            rows = pl.ds(pl.multiple_of(j * block + i * part, part), part)
            left = a[rows, :]
            for which in range(2):
                merged = wbuf[which, rows, :].astype(F32) + mm(left, bpad[which])
                sq[which] += fold_rows(merged * merged)

    marks = sorted(set([0, n] + list(events)))
    for start, end in zip(marks, marks[1:] + [None]):
        for event in events.get(start, []):
            event()
        if end is not None:
            pl.loop(start, end)(norm_step)

    base[...] = jnp.zeros_like(base)
    low[...] = jnp.zeros_like(low)

    def forward(j):
        x = gat[j]
        for which in range(2):
            base[which] += mm(x, wbuf[which, rows_of(j), :])
        low[...] += mm(x, a[rows_of(j), :])

    @pl.loop(0, n // 2)
    def _(q):
        forward(2 * q + core)

    @pl.loop(0, n // 2)
    def _(q):
        origin = 2 * q + 1 - core
        gather_wait(origin)
        forward(origin)

    low_bf = low[...].astype(BF16)
    low_t = jnp.transpose(low[...]).astype(BF16)
    piece = min(256, cols)
    for c0 in range(0, cols, piece):
        cut = slice(c0, c0 + piece)
        norms, scales, bases, pres = [], [], [], []
        for which in range(2):
            norm = jnp.sqrt(jnp.sum(sq[which, :, cut], axis=0, keepdims=True) + 1e-06)
            norms.append(norm)
            scales.append(mag[which : which + 1, cut] / norm)
            bases.append(base[which, :, cut] + mm(low_bf, bpad[which, :, cut]))
            pres.append(bases[which] * scales[which])
        sigma = 1.0 / (1.0 + jnp.exp(-pres[0]))
        hidden[:, cut] = (pres[0] * sigma * pres[1]).astype(BF16)
        cot = gh[:, cut].astype(F32)
        dpres = (
            cot * pres[1] * sigma * (1.0 + pres[0] * (1.0 - sigma)),
            cot * pres[0] * sigma,
        )
        for which in range(2):
            dscaled = (dpres[which] * scales[which]).astype(BF16)
            ds[which, :, cut] = dscaled
            step_m[which : which + 1, cut] = (
                jnp.sum(dpres[which] * bases[which], axis=0, keepdims=True) / norms[which]
            )
            step_b[which, :, cut] = mm(low_t[which * rank : (which + 1) * rank, :], dscaled)

    z0[:tokens, :] = mm_t(ds[0], bpad[0]) + mm_t(ds[1], bpad[1])
    lanes = jnp.zeros((8, width), F32)
    for c0 in range(0, cols, width):
        for which in range(2):
            value = step_b[which, :, c0 : c0 + width]
            lanes += fold_rows(value * value)
            line = step_m[which : which + 1, c0 : c0 + width]
            lanes += jnp.where(
                lax.broadcasted_iota(jnp.int32, (8, width), 0) == 0, line * line, 0.0
            )
    z0[tokens:, :] = lanes

    def start(copy):
        copy.start()
        pending.append(copy)
        return copy

    z_core = start(remote(z0, zc, z_send.at[0], z_recv.at[0], core_peer))

    def partial(j):
        return mm_t(ds[0], wbuf[0, rows_of(j), :]) + mm_t(ds[1], wbuf[1, rows_of(j), :])

    core_copies, mid_copies, hi_copies, z_hi = [], [], [], []
    z_mid = []

    def core_stage(i):
        core_copies[i].wait_recv()
        total = own[i] + rc[i].astype(F32)
        if i < nh:
            sm[i] = total.astype(BF16)
            mid_copies.append(start(remote(sm.at[i], rm.at[i], m_send.at[i], m_recv.at[i], mid_peer)))
        else:
            own[i] = total

    def mid_stage(k):
        mid_copies[k].wait_recv()
        total = own[nh + k] + rm[k].astype(F32)
        if k < nh - 1:
            sh[k] = total.astype(BF16)
            hi_copies.append(
                start(
                    remote(
                        sh.at[k], rh.at[k], h_send.at[k], h_recv.at[k],
                        place(hi_after(k), mid, core),
                    )
                )
            )
        else:
            own[nh + k] = total

    for i in range(2 * nh):
        m = 1 - mid if i < nh else mid
        h = hi_after(i % nh)
        sc[i] = partial(place(h, m, 1 - core)).astype(BF16)
        core_copies.append(start(remote(sc.at[i], rc.at[i], c_send.at[i], c_recv.at[i], core_peer)))
        own[i] = partial(place(h, m, core))
        if i >= 1:
            core_stage(i - 1)
        if i == 1:
            z_core.wait_recv()
            z1[...] = z0[...] + zc[...]
            z_mid.append(start(remote(z1, zm, z_send.at[1], z_recv.at[1], mid_peer)))
        if i == 3:
            z_mid[0].wait_recv()
            zh[hi] = z1[...] + zm[...]
            for k in range(nh - 1):
                z_hi.append(
                    start(
                        remote(
                            zh.at[hi], zh.at[hi], z_send.at[2 + k], z_recv.at[2 + k],
                            place(hi_after(k), mid, core),
                        )
                    )
                )
        if i == nh + 2:
            mid_stage(0)
    core_stage(2 * nh - 1)
    for k in range(1, nh):
        mid_stage(k)

    for k in range(nh - 1):
        slot = hi_before(k)
        remote(zh.at[slot], zh.at[slot], z_send.at[2 + k], z_recv.at[2 + k], core_peer).wait_recv()
    z_sum = zh[0]
    for k in range(1, nh):
        z_sum = z_sum + zh[k]
    z_upper, z_lower = split_parts(z_sum[:tokens, :])
    z_t = jnp.transpose(z_sum[:tokens, :])
    t_upper, t_lower = split_parts(z_t)
    sq[0, :, :width] = z_sum[tokens:, :]

    @pl.loop(0, n)
    def _(j):
        x = gat[j]
        grad = mm(t_upper, x) + mm(t_lower, x)
        folded = fold_rows(grad * grad)
        total = folded[:, :width]
        for c0 in range(width, block, width):
            total += folded[:, c0 : c0 + width]
        sq[0, :, :width] += total

    energy = jnp.sum(jnp.sum(sq[0, :, :width], axis=0, keepdims=True), axis=1, keepdims=True)
    entries = depth * width + 2 * rank * cols * n + 2 * cols * n
    inverse = 1.0 / jnp.sqrt(energy / entries + 1e-06)
    mine = tok[...]
    step_a[...] = jnp.transpose((mm(t_upper, mine) + mm(t_lower, mine)) * inverse)
    step_b[...] = step_b[...] * inverse.reshape(1, 1, 1)
    step_m[...] = step_m[...] * inverse
    a_mine = a[rows_of(me), :]
    total = own[2 * nh - 1] + mm_t(z_upper, a_mine) + mm_t(z_lower, a_mine)
    for k in range(nh - 1):
        hi_copies[k].wait_recv()
        total += rh[k].astype(F32)
    gtok[...] = total.astype(BF16)
    for copy in pending:
        copy.wait_send()


def hand_on(*refs):
    for source, target in zip(refs[:5], refs[5:]):
        target[...] = source[...]


def per_device(n, tokens, grad_hidden, w_gate, w_up, a_factors, b_factors, magnitudes):
    count, block = tokens.shape
    depth, cols = w_gate.shape
    width = a_factors.shape[1]
    nh = n // 4
    vmem = pl.BlockSpec(memory_space=pltpu.VMEM)
    hbm = pl.BlockSpec(memory_space=pl.ANY)
    dma = pltpu.SemaphoreType.DMA
    z_shape = (count + 8, width)
    results = pl.pallas_call(
        functools.partial(kernel, n),
        out_shape=(
            jax.ShapeDtypeStruct((count, cols), BF16),
            jax.ShapeDtypeStruct((count, block), BF16),
            jax.ShapeDtypeStruct((block, width), F32),
            jax.ShapeDtypeStruct((2, width // 2, cols), F32),
            jax.ShapeDtypeStruct((2, cols), F32),
        ),
        in_specs=[vmem, vmem, hbm, hbm, vmem, vmem, vmem],
        out_specs=(vmem,) * 5,
        scratch_shapes=[
            pltpu.VMEM((2, depth, cols), BF16),
            pltpu.VMEM((n, count, block), BF16),
            pltpu.VMEM((2, width, cols), BF16),
            pltpu.VMEM((2, 8, cols), F32),
            pltpu.VMEM((2, count, cols), F32),
            pltpu.VMEM((count, width), F32),
            pltpu.VMEM((2, count, cols), BF16),
            pltpu.VMEM((2 * nh, count, block), F32),
            pltpu.VMEM((2 * nh, count, block), BF16),
            pltpu.VMEM((2 * nh, count, block), BF16),
            pltpu.VMEM((nh, count, block), BF16),
            pltpu.VMEM((nh, count, block), BF16),
            pltpu.VMEM((nh - 1, count, block), BF16),
            pltpu.VMEM((nh - 1, count, block), BF16),
            pltpu.VMEM(z_shape, F32),
            pltpu.VMEM(z_shape, F32),
            pltpu.VMEM(z_shape, F32),
            pltpu.VMEM(z_shape, F32),
            pltpu.VMEM((nh,) + z_shape, F32),
            dma((2, n)),
            dma((n,)),
            dma((n,)),
            dma((2 * nh,)),
            dma((2 * nh,)),
            dma((nh,)),
            dma((nh,)),
            dma((nh - 1,)),
            dma((nh - 1,)),
            dma((nh + 1,)),
            dma((nh + 1,)),
        ],
        compiler_params=pltpu.CompilerParams(
            collective_id=0, has_side_effects=True, vmem_limit_bytes=60 * 1024 * 1024
        ),
    )(tokens, grad_hidden, w_gate, w_up, a_factors, b_factors, magnitudes)
    return pl.pallas_call(
        hand_on,
        out_shape=tuple(jax.ShapeDtypeStruct(r.shape, r.dtype) for r in results),
        in_specs=[vmem] * 5,
        out_specs=(vmem,) * 5,
    )(*results)


def solution(mesh):
    in_specs = (
        P("groups", "out"),
        P("groups", "out"),
        P(None, "out"),
        P(None, "out"),
        P(),
        P(None, None, "out"),
        P(None, "out"),
    )
    out_specs = (
        P("groups", "out"),
        P("groups", "out"),
        P(("groups", "out"), None),
        P("groups", None, "out"),
        P("groups", "out"),
    )
    return jax.shard_map(
        functools.partial(per_device, mesh.shape["out"]),
        mesh=mesh, in_specs=in_specs, out_specs=out_specs, check_vma=False,
    )
```
